32 devices in a mesh: gx: 8 (over z, x), gy: 2 (over y), pa: 2 (over core).
Axes of the slice: x: 2, y: 2, z: 4, core: 2. Of those that a mesh axis runs over, the one named last changes fastest.
Arguments:
- leaf_maps: bfloat16 [8, 2, 2, 1024, 1024], P('gx', 'gy', None, 'pa'), may hold values from -0.125 to 0.125
- face_index: int32 [8, 2, 1024], P('gx', 'gy'), may hold values from 0 to 1023, each once within a row
- order_x: int32 [4, 2], replicated, may hold values from 0 to 1
- order_y: int32 [4, 1], replicated, may hold values from 0 to 1
- traces: float32 [8, 2, 2, 1024], P('gx', 'gy'), may hold values from -6 to 6
Outputs:
- merged_map: bfloat16 [8, 2, 2, 2, 128, 1024], P('gx', 'gy', 'pa')
- outgoing: float32 [8, 2, 2, 2, 128], P('gx', 'gy', 'pa')
The draws below stay inside these ranges and needn't reach their ends.
Inputs may be any that keep to these rules, and one draw needn't show every extreme that they name: `face_index`: each row is a permutation of 0 to 1023.
All inputs are finite; a program needn't handle non-finite values.
Results may differ from the reference program's by a relative error of at most 0.0058.
Values may be sent and summed in bfloat16 or wider, within the bound.
A program may use at most 64 MiB of HBM per device.

```python
import jax
import jax.numpy as jnp
from jax import lax

ORDER = 2048
FC = 1024
NGX = 8
NGY = 2
NBX = 4
NBY = 1
NPA = 2
RW = 128


def plant(entries, stream_key, low, high):
    longest = entries.shape.index(max(entries.shape))
    spots = []
    for shift in (0, 1):
        where = [jax.random.randint(jax.random.fold_in(stream_key, axis), (), 0, length) for axis, length in enumerate(entries.shape)]
        where[longest] = (where[longest] + shift) % entries.shape[longest]
        spots.append(tuple(where))
    return entries.at[spots[0]].set(low).at[spots[1]].set(high)


def shard_levels(own_key, dims, pieces, low, largest):
    level = 1.0
    for position, parts in pieces:
        steps = jax.random.uniform(jax.random.fold_in(jax.random.fold_in(own_key, 6), position), (parts,), jnp.float32, low / len(pieces), largest / len(pieces))
        level = level * jnp.repeat(jnp.exp(steps), dims[position] // parts).reshape((-1,) + (1,) * (len(dims) - 1 - position))
    return level


def noise(stream_key, dims, spread, limit, split=(), held_as=jnp.bfloat16):
    factor_of = shard_levels(stream_key, dims, split, -0.22, 0.18) if split else 1.0
    values = jax.random.normal(stream_key, dims, jnp.float32) * spread * factor_of
    return jnp.minimum(jnp.maximum(values, -limit), limit).astype(held_as)


def setup_inputs(seed: int = 0) -> dict:
    key_of = jax.random.split(jax.random.key(seed), 6)
    return {
        "leaf_maps": noise(key_of[0], (NGX, NGY, 2, FC, FC), ORDER ** -0.5, 0.125, ((0, 8), (1, 2), (3, 2))),
        "face_index": jax.vmap(lambda own: jax.random.permutation(own, FC))(jax.random.split(key_of[1], NGX * NGY)).reshape((NGX, NGY, FC)).astype(jnp.int32),
        "order_x": plant(jax.random.randint(key_of[2], (NBX, NGY), 0, 2), jax.random.fold_in(key_of[2], 1), 0, 1).astype(jnp.int32),
        "order_y": plant(jax.random.randint(key_of[3], (NBX, NBY), 0, 2), jax.random.fold_in(key_of[3], 1), 0, 1).astype(jnp.int32),
        "traces": noise(key_of[4], (NGX, NGY, 2, FC), 1.0, 6.0, ((0, 8), (1, 2)), jnp.float32),
    }


def complex_product(left_panel, right_panel):
    real_part = jnp.dot(left_panel[0], right_panel[0], preferred_element_type=jnp.float32) - jnp.dot(left_panel[1], right_panel[1], preferred_element_type=jnp.float32)
    imag_part = jnp.dot(left_panel[0], right_panel[1], preferred_element_type=jnp.float32) + jnp.dot(left_panel[1], right_panel[0], preferred_element_type=jnp.float32)
    return jnp.stack([real_part, imag_part]).astype(jnp.bfloat16)


def product_pairs(left_stack, right_stack):
    return lax.map(lambda both: complex_product(both[0], both[1]), (left_stack, right_stack))


def reference(leaf_maps, face_index, order_x, order_y, traces):
    index_full = jnp.broadcast_to(face_index[:, :, None, None, :], leaf_maps.shape)
    leaves = jnp.take_along_axis(leaf_maps, index_full, axis=4)
    pairs = leaves.reshape(NBX, 2, NGY, 2, FC, FC)
    chosen = (order_x == 1)[:, :, None, None, None]
    right_one = jnp.where(chosen, pairs[:, 1], pairs[:, 0]).reshape(NBX * NGY, 2, FC, FC)
    left_one = jnp.where(chosen, pairs[:, 0], pairs[:, 1]).reshape(NBX * NGY, 2, FC, FC)
    merged_one = product_pairs(left_one, right_one).reshape(NBX, NBY, 2, 2, FC, FC)
    chosen_two = (order_y == 1)[:, :, None, None, None]
    right_two = jnp.where(chosen_two, merged_one[:, :, 1], merged_one[:, :, 0]).reshape(NBX * NBY, 2, FC, FC)
    left_two = jnp.where(chosen_two, merged_one[:, :, 0], merged_one[:, :, 1]).reshape(NBX * NBY, 2, FC, FC)
    merged_two = product_pairs(left_two, right_two).reshape(NBX, NBY, 2, FC, FC)
    incoming = traces.reshape(NBX, 2, NBY, 2, 2, FC).sum(axis=(1, 3))
    wide = merged_two.astype(jnp.float32)
    hp = lax.Precision.HIGHEST
    real_out = jnp.einsum("ijrc,ijc->ijr", wide[:, :, 0], incoming[:, :, 0], precision=hp) - jnp.einsum("ijrc,ijc->ijr", wide[:, :, 1], incoming[:, :, 1], precision=hp)
    imag_out = jnp.einsum("ijrc,ijc->ijr", wide[:, :, 0], incoming[:, :, 1], precision=hp) + jnp.einsum("ijrc,ijc->ijr", wide[:, :, 1], incoming[:, :, 0], precision=hp)
    box_out = jnp.stack([real_out, imag_out], axis=2)
    laid_map = merged_two.reshape(NBX, NBY, 2, NPA, 2, 2, RW, FC).transpose(0, 4, 1, 5, 3, 2, 6, 7).reshape(NGX, NGY, NPA, 2, RW, FC)
    laid_out = box_out.reshape(NBX, NBY, 2, NPA, 2, 2, RW).transpose(0, 4, 1, 5, 3, 2, 6).reshape(NGX, NGY, NPA, 2, RW)
    return laid_map, laid_out
```

```python
import jax
import jax.numpy as jnp
from jax import lax
from jax.experimental import pallas as pl
from jax.experimental.pallas import tpu as pltpu
from jax.sharding import PartitionSpec as P

MESH = pl.DeviceIdType.MESH
STEPS = 16
LEAD = 2
LAG = 2
BLOCKS = 4
TILE = 256
NT = (((1,), (1,)), ((), ()))


def hot(flags):
    return flags.astype(jnp.float32).astype(jnp.bfloat16)


def mul(left, right):
    return jnp.dot(left, right, preferred_element_type=jnp.float32)


def mul_t(left, right):
    return lax.dot_general(left, right, NT, preferred_element_type=jnp.float32)


def kernel(
    order_x_ref, order_y_ref, leaf_ref, index_ref, trace_ref, map_ref, out_ref,
    raw, index_own, pick, own, outbox, inbox, prod, trace_all, local_sem,
    os, orv, xs, xr, ys, yr, ps, pr, ss, sr,
):
    gx, gy, pa = lax.axis_index("gx"), lax.axis_index("gy"), lax.axis_index("pa")
    half, vert = gx % 2, gy % 2
    other_x, other_y = gx + 1 - 2 * half, gy + 1 - 2 * vert
    ypeer = {"gy": other_y}
    dpeer = {"gx": other_x, "gy": other_y}
    cpeer = {"pa": 1 - pa}
    panel, width = leaf_ref.shape[1], leaf_ref.shape[2]
    rows = map_ref.shape[1]
    quarter = panel // 2
    grain = quarter // STEPS

    barrier = pltpu.get_barrier_semaphore()
    for peer in ({"gx": other_x, "pa": 0}, {"gx": other_x, "pa": 1}, ypeer, dpeer, cpeer):
        pl.semaphore_signal(barrier, inc=1, device_id=peer, device_id_type=MESH)

    load_index = pltpu.make_async_copy(index_ref, index_own, local_sem.at[0])
    load_index.start()
    load_leaf = pltpu.make_async_copy(leaf_ref, raw, local_sem.at[1])
    load_leaf.start()
    load_trace = pltpu.make_async_copy(trace_ref, trace_all.at[0], local_sem.at[2])
    load_trace.start()

    pair, base = gx // 2, gy - vert
    right2 = order_y_ref[gy // 2, pair]
    bit_own = order_x_ref[gy, pair]
    bit_y = order_x_ref[other_y, pair]
    own_left = bit_own != half
    y_left = bit_y != half
    own_second = right2 == vert

    def remote(src, dst, ssem, rsem, peer):
        return pltpu.make_async_remote_copy(
            src_ref=src, dst_ref=dst, send_sem=ssem, recv_sem=rsem,
            device_id=peer, device_id_type=MESH,
        )

    block = panel // BLOCKS

    def own_copy(n):
        part = own.at[:, pa, n * block : (n + 1) * block, :]
        return remote(part, part, os.at[n], orv.at[n], cpeer)

    def x_copy(j, core, source):
        return remote(
            outbox.at[j, core], inbox.at[j, source], xs.at[j, core], xr.at[j, source],
            {"gx": other_x, "pa": core},
        )

    def chunk(slot, j, core):
        start = pl.multiple_of(core * quarter + j * grain, grain)
        return prod.at[slot, :, :, pl.ds(start, grain), :]

    def y_copy(j):
        return remote(chunk(0, j, pa), chunk(1, j, pa), ys.at[j], yr.at[j], ypeer)

    def share(slot, j):
        part = chunk(slot, j, pa)
        return remote(part, part, ps.at[slot, j], pr.at[slot, j], cpeer)

    def trace_copy(n, peer):
        return remote(trace_ref, trace_all.at[n], ss.at[n], sr.at[n], peer)

    traces = [trace_copy(n, peer) for n, peer in ((1, {"gx": other_x}), (2, ypeer), (3, dpeer))]

    load_index.wait()
    index_row = index_own[...]
    for n in range(width // TILE):
        places = lax.broadcasted_iota(jnp.int32, (TILE, width), 0) + n * TILE
        pick[n * TILE : (n + 1) * TILE] = hot(places == index_row)
    load_leaf.wait()

    def permute(n):
        part = raw[:, n * block : (n + 1) * block, :].reshape(2 * block, width)
        value = mul(part, pick[...]).astype(jnp.bfloat16)
        own[:, pa, n * block : (n + 1) * block, :] = value.reshape(2, block, width)

    def stage(j):
        row = lax.broadcasted_iota(jnp.int32, (4 * grain, width), 0)
        core, side, spot = row // (2 * grain), (row // grain) % 2, row % grain
        place = side * panel + core * quarter + j * grain + spot
        unit = hot(lax.broadcasted_iota(jnp.int32, (4 * grain, width), 1) == place)
        for c in range(2):
            turned = mul_t(unit, own[c, pa]).astype(jnp.bfloat16)
            for core in range(2):
                start = pl.multiple_of(core * quarter + j * grain, grain)
                plain = own[c, pa, pl.ds(start, grain), :]
                for side in range(2):
                    at = (2 * core + side) * grain
                    outbox[j, core, c, side * grain : (side + 1) * grain, :] = jnp.where(
                        own_left, plain[:, side * panel : (side + 1) * panel], turned[at : at + grain]
                    )
        for core in range(2):
            x_copy(j, core, pa).start()

    permute(0)
    pl.semaphore_wait(barrier, 5)
    own_copy(0).start()
    for n in range(1, BLOCKS):
        permute(n)
        own_copy(n).start()

    def first(j, carry):
        stage(j)
        return carry

    lax.fori_loop(0, LEAD, first, 0)
    for copy in traces:
        copy.start()
    for n in range(BLOCKS):
        own_copy(n).wait_recv()

    def step(j, carry):
        @pl.when(j < STEPS - LEAD)
        def _():
            stage(j + LEAD)

        for source in range(2):
            x_copy(j, 0, source).wait_recv()
        stack = []
        for c in range(2):
            near = [[inbox[j, b, c, t * grain : (t + 1) * grain, :] for t in range(2)] for b in range(2)]
            stack.append(jnp.concatenate([near[0][0], jnp.where(own_left, near[1][0], near[0][1])], axis=1))
            stack.append(jnp.concatenate([jnp.where(own_left, near[0][1], near[1][0]), near[1][1]], axis=1))
        left = jnp.concatenate(stack, axis=0)
        size = 2 * grain
        start = pl.multiple_of(pa * quarter + j * grain, grain)
        for n in range(width // TILE):
            cols = slice(n * TILE, (n + 1) * TILE)
            here = slice(n * TILE % panel, n * TILE % panel + TILE)
            by = []
            for c in range(2):
                plain = mul(left, own[c, :, :, cols].reshape(width, TILE))
                turned = mul_t(left, own[c, n * TILE // panel, here, :])
                by.append(jnp.where(own_left, turned, plain))
            real = (by[0][:size] - by[1][size:]).astype(jnp.bfloat16)
            imag = (by[1][:size] + by[0][size:]).astype(jnp.bfloat16)
            prod[0, 0, :, pl.ds(start, grain), cols] = real.reshape(2, grain, TILE)
            prod[0, 1, :, pl.ds(start, grain), cols] = imag.reshape(2, grain, TILE)
        y_copy(j).start()
        share(0, j).start()

        @pl.when(j >= LAG)
        def _():
            y_copy(j - LAG).wait_recv()
            share(1, j - LAG).start()

        return carry

    lax.fori_loop(0, STEPS, step, 0)
    for j in range(STEPS - LAG, STEPS):
        y_copy(j).wait_recv()
        share(1, j).start()
    load_trace.wait()
    for copy in traces:
        copy.wait_recv()

    def arrived(j, carry):
        share(0, j).wait_recv()
        share(1, j).wait_recv()
        return carry

    lax.fori_loop(0, STEPS, arrived, 0)

    slot_left = jnp.where(own_second, 1, 0)
    slot_right = 1 - slot_left
    left_turned = jnp.where(own_second, y_left, own_left)
    right_turned = jnp.where(own_second, own_left, y_left)
    within = pl.multiple_of(half * quarter + vert * rows, rows)
    whole = pl.multiple_of(pa * panel + half * quarter + vert * rows, rows)
    unit = hot(
        lax.broadcasted_iota(jnp.int32, (rows, rows), 0) == lax.broadcasted_iota(jnp.int32, (rows, rows), 1)
    )
    stack = []
    for c in range(2):
        plain = prod[slot_left, c, pa, pl.ds(within, rows), :]
        column = prod[slot_left, c, :, :, pl.ds(whole, rows)].reshape(width, rows)
        turned = mul_t(unit, column).astype(jnp.bfloat16)
        stack.append(jnp.where(left_turned, turned, plain))
    left = jnp.concatenate(stack, axis=0)
    for n in range(width // TILE):
        cols = slice(n * TILE, (n + 1) * TILE)
        here = slice(n * TILE % panel, n * TILE % panel + TILE)
        by = []
        for c in range(2):
            plain = mul(left, prod[slot_right, c, :, :, cols].reshape(width, TILE))
            turned = mul_t(left, prod[slot_right, c, n * TILE // panel, here, :])
            by.append(jnp.where(right_turned, turned, plain))
        map_ref[0, :, cols] = (by[0][:rows] - by[1][rows:]).astype(jnp.bfloat16)
        map_ref[1, :, cols] = (by[1][:rows] + by[0][rows:]).astype(jnp.bfloat16)

    trace = (trace_all[0] + trace_all[1]) + (trace_all[2] + trace_all[3])
    wide = map_ref[...].reshape(2 * rows, width).astype(jnp.float32)
    ones = jnp.ones((8, 128), jnp.float32)
    sums = []
    for c in range(2):
        scaled = wide * trace[c : c + 1]
        folded = scaled[:, :128]
        for n in range(1, width // 128):
            folded += scaled[:, n * 128 : (n + 1) * 128]
        sums.append(lax.dot_general(ones, folded, NT, precision=lax.Precision.HIGHEST, preferred_element_type=jnp.float32))
    out_ref[0:1] = sums[0][0:1, :rows] - sums[1][0:1, rows:]
    out_ref[1:2] = sums[1][0:1, :rows] + sums[0][0:1, rows:]

    def sent(j, carry):
        for core in range(2):
            x_copy(j, core, pa).wait_send()
        y_copy(j).wait_send()
        share(0, j).wait_send()
        share(1, j).wait_send()
        return carry

    lax.fori_loop(0, STEPS, sent, 0)
    for n in range(BLOCKS):
        own_copy(n).wait_send()
    for copy in traces:
        copy.wait_send()


def per_device(leaf_maps, face_index, order_x, order_y, traces):
    leaf = leaf_maps[0, 0]
    _, panel, width = leaf.shape
    rows = panel // 4
    grain = panel // 2 // STEPS
    vmem = pl.BlockSpec(memory_space=pltpu.VMEM)
    smem = pl.BlockSpec(memory_space=pltpu.SMEM)
    hbm = pl.BlockSpec(memory_space=pl.ANY)
    dma = pltpu.SemaphoreType.DMA
    merged, outgoing = pl.pallas_call(
        kernel,
        out_shape=(
            pltpu.VMEM((2, rows, width), jnp.bfloat16),
            pltpu.VMEM((2, rows), jnp.float32),
        ),
        in_specs=[smem, smem, hbm, hbm, hbm],
        out_specs=(vmem, vmem),
        scratch_shapes=[
            pltpu.VMEM((2, panel, width), jnp.bfloat16),
            pltpu.VMEM((1, width), jnp.int32),
            pltpu.VMEM((width, width), jnp.bfloat16),
            pltpu.VMEM((2, 2, panel, width), jnp.bfloat16),
            pltpu.VMEM((STEPS, 2, 2, 2 * grain, panel), jnp.bfloat16),
            pltpu.VMEM((STEPS, 2, 2, 2 * grain, panel), jnp.bfloat16),
            pltpu.VMEM((2, 2, 2, panel, width), jnp.bfloat16),
            pltpu.VMEM((4, 2, width), jnp.float32),
            dma((3,)),
            dma((BLOCKS,)), dma((BLOCKS,)),
            dma((STEPS, 2)), dma((STEPS, 2)),
            dma((STEPS,)), dma((STEPS,)),
            dma((2, STEPS)), dma((2, STEPS)),
            dma((4,)), dma((4,)),
        ],
        compiler_params=pltpu.CompilerParams(
            collective_id=0, has_side_effects=True, vmem_limit_bytes=60 * 1024 * 1024
        ),
    )(order_x.T, order_y.T, leaf, face_index[0], traces[0, 0])
    return (
        merged.reshape(1, 1, 1, 2, rows, width),
        outgoing.reshape(1, 1, 1, 2, rows),
    )


def solution(mesh):
    placed = (
        P("gx", "gy", None, "pa", None),
        P("gx", "gy", None),
        P(),
        P(),
        P("gx", "gy", None, None),
    )
    return jax.shard_map(
        per_device,
        mesh=mesh,
        in_specs=placed,
        out_specs=(P("gx", "gy", "pa", None, None, None), P("gx", "gy", "pa", None, None)),
        check_vma=False,
    )
```

```python
import jax
import jax.numpy as jnp
from jax import lax
from jax.experimental import pallas as pl
from jax.experimental.pallas import tpu as pltpu
from jax.sharding import PartitionSpec as P

MESH = pl.DeviceIdType.MESH
STEPS = 16
LEAD = 4
LAG = 2
TILE = 256
NT = (((1,), (1,)), ((), ()))


def hot(flags):
    return flags.astype(jnp.float32).astype(jnp.bfloat16)


def mul(left, right):
    return jnp.dot(left, right, preferred_element_type=jnp.float32)


def mul_t(left, right):
    return lax.dot_general(left, right, NT, preferred_element_type=jnp.float32)


def kernel(
    order_x_ref, order_y_ref, leaf_ref, index_ref, trace_ref, map_ref, out_ref,
    raw, index_own, pick, plain_own, turned_own, factor, outbox, inbox, prod, trace_all, local_sem,
    os, orv, xs, xr, ys, yr, ps, pr, ss, sr,
):
    gx, gy, pa = lax.axis_index("gx"), lax.axis_index("gy"), lax.axis_index("pa")
    half, vert = gx % 2, gy % 2
    other_x, other_y = gx + 1 - 2 * half, gy + 1 - 2 * vert
    ypeer = {"gy": other_y}
    dpeer = {"gx": other_x, "gy": other_y}
    cpeer = {"pa": 1 - pa}
    panel, width = leaf_ref.shape[1], leaf_ref.shape[2]
    rows = map_ref.shape[1]
    quarter = panel // 2
    grain = quarter // STEPS

    barrier = pltpu.get_barrier_semaphore()
    for peer in ({"gx": other_x, "pa": 0}, {"gx": other_x, "pa": 1}, ypeer, dpeer, cpeer):
        pl.semaphore_signal(barrier, inc=1, device_id=peer, device_id_type=MESH)

    load_index = pltpu.make_async_copy(index_ref, index_own, local_sem.at[0])
    load_index.start()
    load_leaf = pltpu.make_async_copy(leaf_ref, raw, local_sem.at[1])
    load_leaf.start()
    load_trace = pltpu.make_async_copy(trace_ref, trace_all.at[0], local_sem.at[2])
    load_trace.start()

    pair, base = gx // 2, gy - vert
    right2 = order_y_ref[gy // 2, pair]
    bit_own = order_x_ref[gy, pair]
    bit_y = order_x_ref[other_y, pair]
    own_left = bit_own != half
    y_left = bit_y != half
    own_second = right2 == vert

    def remote(src, dst, ssem, rsem, peer):
        return pltpu.make_async_remote_copy(
            src_ref=src, dst_ref=dst, send_sem=ssem, recv_sem=rsem,
            device_id=peer, device_id_type=MESH,
        )

    def own_copy(n, c):
        part = factor.at[2 * n + pa, c]
        return remote(part, part, os.at[n, c], orv.at[n, c], cpeer)

    def x_copy(j, core, source):
        return remote(
            outbox.at[j, core], inbox.at[j, source], xs.at[j, core], xr.at[j, source],
            {"gx": other_x, "pa": core},
        )

    def chunk(slot, j, core):
        start = pl.multiple_of(core * quarter + j * grain, grain)
        return prod.at[slot, :, :, pl.ds(start, grain), :]

    def y_copy(j, n):
        start = pl.multiple_of(pa * quarter + j * grain, grain)
        cols = slice(n * panel, (n + 1) * panel)
        return remote(
            prod.at[0, :, :, pl.ds(start, grain), cols], prod.at[1, :, :, pl.ds(start, grain), cols],
            ys.at[j, n], yr.at[j, n], ypeer,
        )

    def share(slot, j):
        part = chunk(slot, j, pa)
        return remote(part, part, ps.at[slot, j], pr.at[slot, j], cpeer)

    def trace_copy(n, peer):
        return remote(trace_ref, trace_all.at[n], ss.at[n], sr.at[n], peer)

    traces = [trace_copy(n, peer) for n, peer in ((1, {"gx": other_x}), (2, ypeer), (3, dpeer))]

    load_index.wait()
    index_row = index_own[...]
    for n in range(width // TILE):
        places = lax.broadcasted_iota(jnp.int32, (TILE, width), 0) + n * TILE
        pick[n * TILE : (n + 1) * TILE] = hot(places == index_row)
    load_leaf.wait()

    def permute(c):
        for n in range(width // TILE):
            cols = slice(n * TILE, (n + 1) * TILE)
            value = mul(raw[c], pick[:, cols]).astype(jnp.bfloat16)
            plain_own[c, :, cols] = value
            turned_own[c, cols, :] = value.T
        for n, which in ((0, pa), (1, 1 - pa)):
            place = pl.ds(pl.multiple_of(which * panel, panel), panel)
            factor[2 * n + pa, c] = jnp.where(own_left, turned_own[c, place, :], plain_own[c, :, place])

    def stage(j):
        for core in range(2):
            for side in range(2):
                start = pl.multiple_of(core * quarter + j * grain, grain)
                deep = pl.multiple_of(side * panel + core * quarter + j * grain, grain)
                outbox[j, core, :, side * grain : (side + 1) * grain, :] = jnp.where(
                    own_left,
                    plain_own[:, pl.ds(start, grain), side * panel : (side + 1) * panel],
                    turned_own[:, pl.ds(deep, grain), :],
                )
        for core in range(2):
            x_copy(j, core, pa).start()

    permute(0)
    pl.semaphore_wait(barrier, 5)
    for n in range(2):
        own_copy(n, 0).start()
    permute(1)
    for n in range(2):
        own_copy(n, 1).start()

    def first(j, carry):
        stage(j)
        return carry

    lax.fori_loop(0, LEAD, first, 0)
    for copy in traces:
        copy.start()
    for n in range(2):
        for c in range(2):
            own_copy(n, c).wait_recv()
    cross = jnp.where(own_left, 3, 2)
    slots = ((0, cross), (5 - cross, 1))

    def step(j, carry):
        @pl.when(j < STEPS - LEAD)
        def _():
            stage(j + LEAD)

        for source in range(2):
            x_copy(j, 0, source).wait_recv()
        stack = []
        for c in range(2):
            near = [[inbox[j, b, c, t * grain : (t + 1) * grain, :] for t in range(2)] for b in range(2)]
            stack.append(jnp.concatenate([near[0][0], jnp.where(own_left, near[1][0], near[0][1])], axis=1))
            stack.append(jnp.concatenate([jnp.where(own_left, near[0][1], near[1][0]), near[1][1]], axis=1))
        left = jnp.concatenate(stack, axis=0)
        size = 2 * grain
        start = pl.multiple_of(pa * quarter + j * grain, grain)
        for side in range(2):
            for n in range(panel // TILE):
                cols = slice(n * TILE, (n + 1) * TILE)
                by = []
                for c in range(2):
                    top = mul(left[:, :panel], factor[slots[0][side], c, :, cols])
                    by.append(top + mul(left[:, panel:], factor[slots[1][side], c, :, cols]))
                real = (by[0][:size] - by[1][size:]).astype(jnp.bfloat16)
                imag = (by[1][:size] + by[0][size:]).astype(jnp.bfloat16)
                cols = slice(side * panel + n * TILE, side * panel + (n + 1) * TILE)
                prod[0, 0, :, pl.ds(start, grain), cols] = real.reshape(2, grain, TILE)
                prod[0, 1, :, pl.ds(start, grain), cols] = imag.reshape(2, grain, TILE)
            y_copy(j, side).start()
        share(0, j).start()

        @pl.when(j >= LAG)
        def _():
            for n in range(2):
                y_copy(j - LAG, n).wait_recv()
            share(1, j - LAG).start()

        return carry

    lax.fori_loop(0, STEPS, step, 0)
    for j in range(STEPS - LAG, STEPS):
        for n in range(2):
            y_copy(j, n).wait_recv()
        share(1, j).start()
    load_trace.wait()
    for copy in traces:
        copy.wait_recv()

    def arrived(j, carry):
        share(0, j).wait_recv()
        share(1, j).wait_recv()
        return carry

    lax.fori_loop(0, STEPS, arrived, 0)

    slot_left = jnp.where(own_second, 1, 0)
    slot_right = 1 - slot_left
    left_turned = jnp.where(own_second, y_left, own_left)
    right_turned = jnp.where(own_second, own_left, y_left)
    within = pl.multiple_of(half * quarter + vert * rows, rows)
    whole = pl.multiple_of(pa * panel + half * quarter + vert * rows, rows)
    across, down = [], []
    for c in range(2):
        plain = prod[slot_left, c, pa, pl.ds(within, rows), :]
        column = prod[slot_left, c, :, :, pl.ds(whole, rows)].reshape(width, rows)
        across.append(jnp.where(left_turned, column.T, plain))
        down.append(jnp.where(left_turned, column, plain.T))
    left = jnp.concatenate(across, axis=0)
    right = jnp.concatenate(down, axis=1)
    for n in range(width // TILE):
        cols = slice(n * TILE, (n + 1) * TILE)
        here = slice(n * TILE % panel, n * TILE % panel + TILE)
        by = [mul(left, prod[slot_right, c, :, :, cols].reshape(width, TILE)) for c in range(2)]
        to = [mul(prod[slot_right, c, n * TILE // panel, here, :], right) for c in range(2)]
        real = (by[0][:rows] - by[1][rows:]).astype(jnp.bfloat16)
        imag = (by[1][:rows] + by[0][rows:]).astype(jnp.bfloat16)
        real_t = (to[0][:, :rows] - to[1][:, rows:]).astype(jnp.bfloat16)
        imag_t = (to[1][:, :rows] + to[0][:, rows:]).astype(jnp.bfloat16)
        map_ref[0, :, cols] = jnp.where(right_turned, real_t.T, real)
        map_ref[1, :, cols] = jnp.where(right_turned, imag_t.T, imag)

    trace = (trace_all[0] + trace_all[1]) + (trace_all[2] + trace_all[3])
    wide = map_ref[...].reshape(2 * rows, width).astype(jnp.float32)
    ones = jnp.ones((8, 128), jnp.float32)
    sums = []
    for c in range(2):
        scaled = wide * trace[c : c + 1]
        folded = scaled[:, :128]
        for n in range(1, width // 128):
            folded += scaled[:, n * 128 : (n + 1) * 128]
        sums.append(lax.dot_general(ones, folded, NT, precision=lax.Precision.HIGHEST, preferred_element_type=jnp.float32))
    out_ref[0:1] = sums[0][0:1, :rows] - sums[1][0:1, rows:]
    out_ref[1:2] = sums[1][0:1, :rows] + sums[0][0:1, rows:]

    def sent(j, carry):
        for core in range(2):
            x_copy(j, core, pa).wait_send()
        for n in range(2):
            y_copy(j, n).wait_send()
        share(0, j).wait_send()
        share(1, j).wait_send()
        return carry

    lax.fori_loop(0, STEPS, sent, 0)
    for n in range(2):
        for c in range(2):
            own_copy(n, c).wait_send()
    for copy in traces:
        copy.wait_send()


def per_device(leaf_maps, face_index, order_x, order_y, traces):
    leaf = leaf_maps[0, 0]
    _, panel, width = leaf.shape
    rows = panel // 4
    grain = panel // 2 // STEPS
    vmem = pl.BlockSpec(memory_space=pltpu.VMEM)
    smem = pl.BlockSpec(memory_space=pltpu.SMEM)
    hbm = pl.BlockSpec(memory_space=pl.ANY)
    dma = pltpu.SemaphoreType.DMA
    merged, outgoing = pl.pallas_call(
        kernel,
        out_shape=(
            pltpu.VMEM((2, rows, width), jnp.bfloat16),
            pltpu.VMEM((2, rows), jnp.float32),
        ),
        in_specs=[smem, smem, hbm, hbm, hbm],
        out_specs=(vmem, vmem),
        scratch_shapes=[
            pltpu.VMEM((2, panel, width), jnp.bfloat16),
            pltpu.VMEM((1, width), jnp.int32),
            pltpu.VMEM((width, width), jnp.bfloat16),
            pltpu.VMEM((2, panel, width), jnp.bfloat16),
            pltpu.VMEM((2, width, panel), jnp.bfloat16),
            pltpu.VMEM((4, 2, panel, panel), jnp.bfloat16),
            pltpu.VMEM((STEPS, 2, 2, 2 * grain, panel), jnp.bfloat16),
            pltpu.VMEM((STEPS, 2, 2, 2 * grain, panel), jnp.bfloat16),
            pltpu.VMEM((2, 2, 2, panel, width), jnp.bfloat16),
            pltpu.VMEM((4, 2, width), jnp.float32),
            dma((3,)),
            dma((2, 2)), dma((2, 2)),
            dma((STEPS, 2)), dma((STEPS, 2)),
            dma((STEPS, 2)), dma((STEPS, 2)),
            dma((2, STEPS)), dma((2, STEPS)),
            dma((4,)), dma((4,)),
        ],
        compiler_params=pltpu.CompilerParams(
            collective_id=0, has_side_effects=True, vmem_limit_bytes=60 * 1024 * 1024
        ),
    )(order_x.T, order_y.T, leaf, face_index[0], traces[0, 0])
    return (
        merged.reshape(1, 1, 1, 2, rows, width),
        outgoing.reshape(1, 1, 1, 2, rows),
    )


def solution(mesh):
    placed = (
        P("gx", "gy", None, "pa", None),
        P("gx", "gy", None),
        P(),
        P(),
        P("gx", "gy", None, None),
    )
    return jax.shard_map(
        per_device,
        mesh=mesh,
        in_specs=placed,
        out_specs=(P("gx", "gy", "pa", None, None, None), P("gx", "gy", "pa", None, None)),
        check_vma=False,
    )
```

```python
import jax
import jax.numpy as jnp
from jax import lax
from jax.experimental import pallas as pl
from jax.experimental.pallas import tpu as pltpu
from jax.sharding import PartitionSpec as P

MESH = pl.DeviceIdType.MESH
STEPS = 16
LEAD = 4
LAG = 2
GROUP = 4
TILE = 256
NT = (((1,), (1,)), ((), ()))


def hot(flags):
    return flags.astype(jnp.float32).astype(jnp.bfloat16)


def mul(left, right):
    return jnp.dot(left, right, preferred_element_type=jnp.float32)


def mul_t(left, right):
    return lax.dot_general(left, right, NT, preferred_element_type=jnp.float32)


def kernel(
    order_x_ref, order_y_ref, leaf_ref, index_ref, trace_ref, map_ref, out_ref,
    raw, index_own, pick, plain_own, turned_own, factor, outbox, inbox, prod, trace_all, local_sem,
    os, orv, xs, xr, ys, yr, ps, pr, ss, sr,
):
    gx, gy, pa = lax.axis_index("gx"), lax.axis_index("gy"), lax.axis_index("pa")
    half, vert = gx % 2, gy % 2
    other_x, other_y = gx + 1 - 2 * half, gy + 1 - 2 * vert
    ypeer = {"gy": other_y}
    dpeer = {"gx": other_x, "gy": other_y}
    cpeer = {"pa": 1 - pa}
    panel, width = leaf_ref.shape[1], leaf_ref.shape[2]
    rows = map_ref.shape[1]
    quarter = panel // 2
    grain = quarter // STEPS

    barrier = pltpu.get_barrier_semaphore()
    for peer in ({"gx": other_x, "pa": 0}, {"gx": other_x, "pa": 1}, ypeer, dpeer, cpeer):
        pl.semaphore_signal(barrier, inc=1, device_id=peer, device_id_type=MESH)

    load_index = pltpu.make_async_copy(index_ref, index_own, local_sem.at[0])
    load_index.start()
    load_leaf = pltpu.make_async_copy(leaf_ref, raw, local_sem.at[1])
    load_leaf.start()
    load_trace = pltpu.make_async_copy(trace_ref, trace_all.at[0], local_sem.at[2])
    load_trace.start()

    pair, base = gx // 2, gy - vert
    right2 = order_y_ref[gy // 2, pair]
    bit_own = order_x_ref[gy, pair]
    bit_y = order_x_ref[other_y, pair]
    own_left = bit_own != half
    y_left = bit_y != half
    own_second = right2 == vert

    def remote(src, dst, ssem, rsem, peer):
        return pltpu.make_async_remote_copy(
            src_ref=src, dst_ref=dst, send_sem=ssem, recv_sem=rsem,
            device_id=peer, device_id_type=MESH,
        )

    def own_copy(n, c):
        part = factor.at[2 * n + pa, c]
        return remote(part, part, os.at[n, c], orv.at[n, c], cpeer)

    def x_copy(j, core, source):
        return remote(
            outbox.at[j, core], inbox.at[j, source], xs.at[j, core], xr.at[j, source],
            {"gx": other_x, "pa": core},
        )

    def y_copy(j, n):
        start = pl.multiple_of(pa * quarter + j * grain, grain)
        cols = slice(n * panel, (n + 1) * panel)
        return remote(
            prod.at[0, :, :, pl.ds(start, grain), cols], prod.at[1, :, :, pl.ds(start, grain), cols],
            ys.at[j, n], yr.at[j, n], ypeer,
        )

    def share(slot, j, n):
        start = pl.multiple_of(pa * quarter + j * grain, grain)
        part = prod.at[slot, :, :, pl.ds(start, n * grain), :]
        return remote(part, part, ps.at[slot, j], pr.at[slot, j], cpeer)

    def finish(j):
        for core in range(2):
            x_copy(j, core, pa).wait_send()
        for n in range(2):
            y_copy(j, n).wait_send()

    def trace_copy(n, peer):
        return remote(trace_ref, trace_all.at[n], ss.at[n], sr.at[n], peer)

    traces = [trace_copy(n, peer) for n, peer in ((1, {"gx": other_x}), (2, ypeer), (3, dpeer))]

    load_index.wait()
    index_row = index_own[...]
    for n in range(width // TILE):
        places = lax.broadcasted_iota(jnp.int32, (TILE, width), 0) + n * TILE
        pick[n * TILE : (n + 1) * TILE] = hot(places == index_row)
    load_leaf.wait()

    def permute(c):
        for n in range(width // TILE):
            cols = slice(n * TILE, (n + 1) * TILE)
            value = mul(raw[c], pick[:, cols]).astype(jnp.bfloat16)
            plain_own[c, :, cols] = value
            turned_own[c, cols, :] = value.T
        for n, which in ((0, pa), (1, 1 - pa)):
            place = pl.ds(pl.multiple_of(which * panel, panel), panel)
            factor[2 * n + pa, c] = jnp.where(own_left, turned_own[c, place, :], plain_own[c, :, place])

    def lay(j, c):
        for core in range(2):
            for side in range(2):
                start = pl.multiple_of(core * quarter + j * grain, grain)
                deep = pl.multiple_of(side * panel + core * quarter + j * grain, grain)
                outbox[j, core, c, side * grain : (side + 1) * grain, :] = jnp.where(
                    own_left,
                    plain_own[c, pl.ds(start, grain), side * panel : (side + 1) * panel],
                    turned_own[c, pl.ds(deep, grain), :],
                )

    def stage(j):
        lay(j, 0)
        lay(j, 1)
        for core in range(2):
            x_copy(j, core, pa).start()

    def opening(c):
        permute(c)
        lay(0, c)
        if c == 0:
            pl.semaphore_wait(barrier, 5)
        for core in range(2):
            remote(
                outbox.at[0, core, c], inbox.at[0, pa, c], xs.at[0, core], xr.at[0, pa],
                {"gx": other_x, "pa": core},
            ).start()
        for n in range(2):
            own_copy(n, c).start()

    opening(0)
    opening(1)

    def first(j, carry):
        stage(j)
        return carry

    lax.fori_loop(1, LEAD, first, 0)
    for copy in traces:
        copy.start()
    for n in range(2):
        for c in range(2):
            own_copy(n, c).wait_recv()
    cross = jnp.where(own_left, 3, 2)
    slots = ((0, cross), (5 - cross, 1))

    def step(j, carry):
        @pl.when(j < STEPS - LEAD)
        def _():
            stage(j + LEAD)

        for source in range(2):
            x_copy(j, 0, source).wait_recv()
        stack = []
        for c in range(2):
            near = [[inbox[j, b, c, t * grain : (t + 1) * grain, :] for t in range(2)] for b in range(2)]
            stack.append(jnp.concatenate([near[0][0], jnp.where(own_left, near[1][0], near[0][1])], axis=1))
            stack.append(jnp.concatenate([jnp.where(own_left, near[0][1], near[1][0]), near[1][1]], axis=1))
        left = jnp.concatenate(stack, axis=0)
        size = 2 * grain
        start = pl.multiple_of(pa * quarter + j * grain, grain)
        for side in range(2):
            for n in range(panel // TILE):
                cols = slice(n * TILE, (n + 1) * TILE)
                by = []
                for c in range(2):
                    top = mul(left[:, :panel], factor[slots[0][side], c, :, cols])
                    by.append(top + mul(left[:, panel:], factor[slots[1][side], c, :, cols]))
                real = (by[0][:size] - by[1][size:]).astype(jnp.bfloat16)
                imag = (by[1][:size] + by[0][size:]).astype(jnp.bfloat16)
                cols = slice(side * panel + n * TILE, side * panel + (n + 1) * TILE)
                prod[0, 0, :, pl.ds(start, grain), cols] = real.reshape(2, grain, TILE)
                prod[0, 1, :, pl.ds(start, grain), cols] = imag.reshape(2, grain, TILE)
            y_copy(j, side).start()

        @pl.when(j % GROUP == GROUP - 1)
        def _():
            share(0, j + 1 - GROUP, GROUP).start()

            @pl.when(j >= GROUP)
            def _():
                share(0, j + 1 - 2 * GROUP, GROUP).wait()

        @pl.when(j >= GROUP)
        def _():
            finish(j - GROUP)

        @pl.when(j >= LAG)
        def _():
            for n in range(2):
                y_copy(j - LAG, n).wait_recv()

        @pl.when((j >= LAG) & ((j - LAG) % GROUP == GROUP - 1))
        def _():
            share(1, j - LAG + 1 - GROUP, GROUP).start()

            @pl.when(j - LAG >= GROUP)
            def _():
                share(1, j - LAG + 1 - 2 * GROUP, GROUP).wait()

        return carry

    lax.fori_loop(0, STEPS, step, 0)
    rest = [share(0, STEPS - GROUP, GROUP), share(1, STEPS - 2 * GROUP, GROUP)]
    tail = share(1, STEPS - GROUP, GROUP - LAG)
    tail.start()
    rest.append(tail)
    for j in range(STEPS - LAG, STEPS):
        for n in range(2):
            y_copy(j, n).wait_recv()
        tail = share(1, j, 1)
        tail.start()
        rest.append(tail)
    for j in range(STEPS - GROUP, STEPS):
        finish(j)
    load_trace.wait()
    for copy in traces:
        copy.wait()
    for n in range(2):
        for c in range(2):
            own_copy(n, c).wait_send()
    for copy in rest:
        copy.wait()

    slot_left = jnp.where(own_second, 1, 0)
    slot_right = 1 - slot_left
    left_turned = jnp.where(own_second, y_left, own_left)
    right_turned = jnp.where(own_second, own_left, y_left)
    within = pl.multiple_of(half * quarter + vert * rows, rows)
    whole = pl.multiple_of(pa * panel + half * quarter + vert * rows, rows)
    across, down = [], []
    for c in range(2):
        plain = prod[slot_left, c, pa, pl.ds(within, rows), :]
        column = prod[slot_left, c, :, :, pl.ds(whole, rows)].reshape(width, rows)
        across.append(jnp.where(left_turned, column.T, plain))
        down.append(jnp.where(left_turned, column, plain.T))
    left = jnp.concatenate(across, axis=0)
    right = jnp.concatenate(down, axis=1)
    trace = (trace_all[0] + trace_all[1]) + (trace_all[2] + trace_all[3])
    folded = [[None, None], [None, None]]
    for n in range(width // TILE):
        cols = slice(n * TILE, (n + 1) * TILE)
        here = slice(n * TILE % panel, n * TILE % panel + TILE)
        by = [mul(left, prod[slot_right, c, :, :, cols].reshape(width, TILE)) for c in range(2)]
        to = [mul(prod[slot_right, c, n * TILE // panel, here, :], right) for c in range(2)]
        real = (by[0][:rows] - by[1][rows:]).astype(jnp.bfloat16)
        imag = (by[1][:rows] + by[0][rows:]).astype(jnp.bfloat16)
        real_t = (to[0][:, :rows] - to[1][:, rows:]).astype(jnp.bfloat16)
        imag_t = (to[1][:, :rows] + to[0][:, rows:]).astype(jnp.bfloat16)
        for part, value in enumerate((jnp.where(right_turned, real_t.T, real), jnp.where(right_turned, imag_t.T, imag))):
            map_ref[part, :, cols] = value
            wide = value.astype(jnp.float32)
            for c in range(2):
                scaled = wide * trace[c : c + 1, cols]
                for m in range(TILE // 128):
                    term = scaled[:, m * 128 : (m + 1) * 128]
                    folded[c][part] = term if folded[c][part] is None else folded[c][part] + term

    ones = jnp.ones((8, 128), jnp.float32)
    sums = [
        lax.dot_general(
            ones, jnp.concatenate(folded[c], axis=0), NT,
            precision=lax.Precision.HIGHEST, preferred_element_type=jnp.float32,
        )
        for c in range(2)
    ]
    out_ref[0:1] = sums[0][0:1, :rows] - sums[1][0:1, rows:]
    out_ref[1:2] = sums[1][0:1, :rows] + sums[0][0:1, rows:]


def per_device(leaf_maps, face_index, order_x, order_y, traces):
    leaf = leaf_maps[0, 0]
    _, panel, width = leaf.shape
    rows = panel // 4
    grain = panel // 2 // STEPS
    vmem = pl.BlockSpec(memory_space=pltpu.VMEM)
    smem = pl.BlockSpec(memory_space=pltpu.SMEM)
    hbm = pl.BlockSpec(memory_space=pl.ANY)
    dma = pltpu.SemaphoreType.DMA
    merged, outgoing = pl.pallas_call(
        kernel,
        out_shape=(
            pltpu.VMEM((2, rows, width), jnp.bfloat16),
            pltpu.VMEM((2, rows), jnp.float32),
        ),
        in_specs=[smem, smem, hbm, hbm, hbm],
        out_specs=(vmem, vmem),
        scratch_shapes=[
            pltpu.VMEM((2, panel, width), jnp.bfloat16),
            pltpu.VMEM((1, width), jnp.int32),
            pltpu.VMEM((width, width), jnp.bfloat16),
            pltpu.VMEM((2, panel, width), jnp.bfloat16),
            pltpu.VMEM((2, width, panel), jnp.bfloat16),
            pltpu.VMEM((4, 2, panel, panel), jnp.bfloat16),
            pltpu.VMEM((STEPS, 2, 2, 2 * grain, panel), jnp.bfloat16),
            pltpu.VMEM((STEPS, 2, 2, 2 * grain, panel), jnp.bfloat16),
            pltpu.VMEM((2, 2, 2, panel, width), jnp.bfloat16),
            pltpu.VMEM((4, 2, width), jnp.float32),
            dma((3,)),
            dma((2, 2)), dma((2, 2)),
            dma((STEPS, 2)), dma((STEPS, 2)),
            dma((STEPS, 2)), dma((STEPS, 2)),
            dma((2, STEPS)), dma((2, STEPS)),
            dma((4,)), dma((4,)),
        ],
        compiler_params=pltpu.CompilerParams(
            collective_id=0, has_side_effects=True, vmem_limit_bytes=60 * 1024 * 1024
        ),
    )(order_x.T, order_y.T, leaf, face_index[0], traces[0, 0])
    return (
        merged.reshape(1, 1, 1, 2, rows, width),
        outgoing.reshape(1, 1, 1, 2, rows),
    )


def solution(mesh):
    placed = (
        P("gx", "gy", None, "pa", None),
        P("gx", "gy", None),
        P(),
        P(),
        P("gx", "gy", None, None),
    )
    return jax.shard_map(
        per_device,
        mesh=mesh,
        in_specs=placed,
        out_specs=(P("gx", "gy", "pa", None, None, None), P("gx", "gy", "pa", None, None)),
        check_vma=False,
    )
```

```python
import jax
import jax.numpy as jnp
from jax import lax
from jax.experimental import pallas as pl
from jax.experimental.pallas import tpu as pltpu
from jax.sharding import PartitionSpec as P

MESH = pl.DeviceIdType.MESH
STEPS = 16
LEAD = 4
LAG = 2
GROUP = 4
TILE = 512
NT = (((1,), (1,)), ((), ()))


def hot(flags):
    return flags.astype(jnp.float32).astype(jnp.bfloat16)


def mul(left, right):
    return jnp.dot(left, right, preferred_element_type=jnp.float32)


def mul_t(left, right):
    return lax.dot_general(left, right, NT, preferred_element_type=jnp.float32)


def kernel(
    order_x_ref, order_y_ref, leaf_ref, index_ref, trace_ref, map_ref, out_ref,
    raw, index_own, pick, plain_own, turned_own, factor, outbox, inbox, prod, trace_all, local_sem,
    os, orv, xs, xr, ys, yr, ps, pr, ss, sr,
):
    gx, gy, pa = lax.axis_index("gx"), lax.axis_index("gy"), lax.axis_index("pa")
    half, vert = gx % 2, gy % 2
    other_x, other_y = gx + 1 - 2 * half, gy + 1 - 2 * vert
    ypeer = {"gy": other_y}
    dpeer = {"gx": other_x, "gy": other_y}
    cpeer = {"pa": 1 - pa}
    panel, width = leaf_ref.shape[1], leaf_ref.shape[2]
    rows = map_ref.shape[1]
    quarter = panel // 2
    grain = quarter // STEPS

    barrier = pltpu.get_barrier_semaphore()
    for peer in ({"gx": other_x, "pa": 0}, {"gx": other_x, "pa": 1}, ypeer, dpeer, cpeer):
        pl.semaphore_signal(barrier, inc=1, device_id=peer, device_id_type=MESH)

    load_index = pltpu.make_async_copy(index_ref, index_own, local_sem.at[0])
    load_index.start()
    load_leaf = pltpu.make_async_copy(leaf_ref, raw, local_sem.at[1])
    load_leaf.start()
    load_trace = pltpu.make_async_copy(trace_ref, trace_all.at[0], local_sem.at[2])
    load_trace.start()

    pair, base = gx // 2, gy - vert
    right2 = order_y_ref[gy // 2, pair]
    bit_own = order_x_ref[gy, pair]
    bit_y = order_x_ref[other_y, pair]
    own_left = bit_own != half
    y_left = bit_y != half
    own_second = right2 == vert

    def remote(src, dst, ssem, rsem, peer):
        return pltpu.make_async_remote_copy(
            src_ref=src, dst_ref=dst, send_sem=ssem, recv_sem=rsem,
            device_id=peer, device_id_type=MESH,
        )

    def own_copy(n, c):
        part = factor.at[2 * n + pa, c]
        return remote(part, part, os.at[n, c], orv.at[n, c], cpeer)

    def x_copy(j, core, source):
        return remote(
            outbox.at[j, core], inbox.at[j, source], xs.at[j, core], xr.at[j, source],
            {"gx": other_x, "pa": core},
        )

    def y_copy(j, n, size=1):
        start = pl.multiple_of(pa * quarter + j * grain, grain)
        cols = slice(n * panel, (n + size) * panel)
        return remote(
            prod.at[0, :, :, pl.ds(start, grain), cols], prod.at[1, :, :, pl.ds(start, grain), cols],
            ys.at[j], yr.at[j], ypeer,
        )

    def share(slot, j, n):
        start = pl.multiple_of(pa * quarter + j * grain, grain)
        part = prod.at[slot, :, :, pl.ds(start, n * grain), :]
        return remote(part, part, ps.at[slot, j], pr.at[slot, j], cpeer)

    def finish(j):
        for core in range(2):
            x_copy(j, core, pa).wait_send()
        y_copy(j, 0, 2).wait_send()

    def trace_copy(n, peer):
        return remote(trace_ref, trace_all.at[n], ss.at[n], sr.at[n], peer)

    traces = [trace_copy(n, peer) for n, peer in ((1, {"gx": other_x}), (2, ypeer), (3, dpeer))]

    load_index.wait()
    index_row = index_own[...]
    for n in range(width // TILE):
        places = lax.broadcasted_iota(jnp.int32, (TILE, width), 0) + n * TILE
        pick[n * TILE : (n + 1) * TILE] = hot(places == index_row)
    load_leaf.wait()

    def permute(c):
        for n in range(width // TILE):
            cols = slice(n * TILE, (n + 1) * TILE)
            value = mul(raw[c], pick[:, cols]).astype(jnp.bfloat16)
            plain_own[c, :, cols] = value
            turned_own[c, cols, :] = value.T
    def choose(n, which, c):
        place = pl.ds(pl.multiple_of(which * panel, panel), panel)
        factor[2 * n + pa, c] = jnp.where(own_left, turned_own[c, place, :], plain_own[c, :, place])
        own_copy(n, c).start()

    def lay(j, c):
        for core in range(2):
            for side in range(2):
                start = pl.multiple_of(core * quarter + j * grain, grain)
                deep = pl.multiple_of(side * panel + core * quarter + j * grain, grain)
                outbox[j, core, c, side * grain : (side + 1) * grain, :] = jnp.where(
                    own_left,
                    plain_own[c, pl.ds(start, grain), side * panel : (side + 1) * panel],
                    turned_own[c, pl.ds(deep, grain), :],
                )

    def stage(j):
        lay(j, 0)
        lay(j, 1)
        for core in range(2):
            x_copy(j, core, pa).start()

    def opening(c):
        permute(c)
        lay(0, c)
        if c == 0:
            pl.semaphore_wait(barrier, 5)
        for core in range(2):
            remote(
                outbox.at[0, core, c], inbox.at[0, pa, c], xs.at[0, core], xr.at[0, pa],
                {"gx": other_x, "pa": core},
            ).start()
        choose(0, pa, c)
        choose(1, 1 - pa, c)

    opening(0)
    opening(1)

    def first(j, carry):
        stage(j)
        return carry

    lax.fori_loop(1, LEAD, first, 0)
    for copy in traces:
        copy.start()
    for n in range(2):
        for c in range(2):
            own_copy(n, c).wait_recv()
    cross = jnp.where(own_left, 3, 2)
    slots = ((0, cross), (5 - cross, 1))

    def step(j, carry):
        @pl.when(j < STEPS - LEAD)
        def _():
            stage(j + LEAD)

        for source in range(2):
            x_copy(j, 0, source).wait_recv()
        stack = []
        for c in range(2):
            near = [[inbox[j, b, c, t * grain : (t + 1) * grain, :] for t in range(2)] for b in range(2)]
            stack.append(jnp.concatenate([near[0][0], jnp.where(own_left, near[1][0], near[0][1])], axis=1))
            stack.append(jnp.concatenate([jnp.where(own_left, near[0][1], near[1][0]), near[1][1]], axis=1))
        left = jnp.concatenate(stack, axis=0)
        size = 2 * grain
        start = pl.multiple_of(pa * quarter + j * grain, grain)
        for side in range(2):
            for n in range(panel // TILE):
                cols = slice(n * TILE, (n + 1) * TILE)
                by = []
                for c in range(2):
                    top = mul(left[:, :panel], factor[slots[0][side], c, :, cols])
                    by.append(top + mul(left[:, panel:], factor[slots[1][side], c, :, cols]))
                real = (by[0][:size] - by[1][size:]).astype(jnp.bfloat16)
                imag = (by[1][:size] + by[0][size:]).astype(jnp.bfloat16)
                cols = slice(side * panel + n * TILE, side * panel + (n + 1) * TILE)
                prod[0, 0, :, pl.ds(start, grain), cols] = real.reshape(2, grain, TILE)
                prod[0, 1, :, pl.ds(start, grain), cols] = imag.reshape(2, grain, TILE)
            @pl.when((j == 0) | (j == STEPS - 1))
            def _(side=side):
                y_copy(j, side).start()

            if side:
                @pl.when((j > 0) & (j < STEPS - 1))
                def _():
                    y_copy(j, 0, 2).start()


        @pl.when(j % GROUP == GROUP - 1)
        def _():
            share(0, j + 1 - GROUP, GROUP).start()

            @pl.when(j >= GROUP)
            def _():
                share(0, j + 1 - 2 * GROUP, GROUP).wait()

        @pl.when(j >= GROUP)
        def _():
            finish(j - GROUP)

        @pl.when(j >= LAG)
        def _():
            y_copy(j - LAG, 0, 2).wait_recv()

        @pl.when((j >= LAG) & ((j - LAG) % GROUP == GROUP - 1))
        def _():
            share(1, j - LAG + 1 - GROUP, GROUP).start()

            @pl.when(j - LAG >= GROUP)
            def _():
                share(1, j - LAG + 1 - 2 * GROUP, GROUP).wait()

        return carry

    lax.fori_loop(0, STEPS, step, 0)
    rest = [share(0, STEPS - GROUP, GROUP), share(1, STEPS - 2 * GROUP, GROUP)]
    tail = share(1, STEPS - GROUP, GROUP - LAG)
    tail.start()
    rest.append(tail)
    for j in range(STEPS - LAG, STEPS):
        y_copy(j, 0, 2).wait_recv()
        tail = share(1, j, 1)
        tail.start()
        rest.append(tail)
    for j in range(STEPS - GROUP, STEPS):
        finish(j)
    load_trace.wait()
    for copy in traces:
        copy.wait()
    for n in range(2):
        for c in range(2):
            own_copy(n, c).wait_send()
    for copy in rest:
        copy.wait()

    slot_left = jnp.where(own_second, 1, 0)
    slot_right = 1 - slot_left
    left_turned = jnp.where(own_second, y_left, own_left)
    right_turned = jnp.where(own_second, own_left, y_left)
    within = pl.multiple_of(half * quarter + vert * rows, rows)
    whole = pl.multiple_of(pa * panel + half * quarter + vert * rows, rows)
    across, down = [], []
    for c in range(2):
        plain = prod[slot_left, c, pa, pl.ds(within, rows), :]
        column = prod[slot_left, c, :, :, pl.ds(whole, rows)].reshape(width, rows)
        across.append(jnp.where(left_turned, column.T, plain))
        down.append(jnp.where(left_turned, column, plain.T))
    left = jnp.concatenate(across, axis=0)
    right = jnp.concatenate(down, axis=1)
    trace = (trace_all[0] + trace_all[1]) + (trace_all[2] + trace_all[3])
    folded = [[None, None], [None, None]]
    for n in range(width // TILE):
        cols = slice(n * TILE, (n + 1) * TILE)
        here = slice(n * TILE % panel, n * TILE % panel + TILE)
        by = [mul(left, prod[slot_right, c, :, :, cols].reshape(width, TILE)) for c in range(2)]
        to = [mul(prod[slot_right, c, n * TILE // panel, here, :], right) for c in range(2)]
        real = (by[0][:rows] - by[1][rows:]).astype(jnp.bfloat16)
        imag = (by[1][:rows] + by[0][rows:]).astype(jnp.bfloat16)
        real_t = (to[0][:, :rows] - to[1][:, rows:]).astype(jnp.bfloat16)
        imag_t = (to[1][:, :rows] + to[0][:, rows:]).astype(jnp.bfloat16)
        for part, value in enumerate((jnp.where(right_turned, real_t.T, real), jnp.where(right_turned, imag_t.T, imag))):
            map_ref[part, :, cols] = value
            wide = value.astype(jnp.float32)
            for c in range(2):
                scaled = wide * trace[c : c + 1, cols]
                for m in range(TILE // 128):
                    term = scaled[:, m * 128 : (m + 1) * 128]
                    folded[c][part] = term if folded[c][part] is None else folded[c][part] + term

    ones = jnp.ones((8, 128), jnp.float32)
    sums = [
        lax.dot_general(
            ones, jnp.concatenate(folded[c], axis=0), NT,
            precision=lax.Precision.HIGHEST, preferred_element_type=jnp.float32,
        )
        for c in range(2)
    ]
    out_ref[0:1] = sums[0][0:1, :rows] - sums[1][0:1, rows:]
    out_ref[1:2] = sums[1][0:1, :rows] + sums[0][0:1, rows:]


def per_device(leaf_maps, face_index, order_x, order_y, traces):
    leaf = leaf_maps[0, 0]
    _, panel, width = leaf.shape
    rows = panel // 4
    grain = panel // 2 // STEPS
    vmem = pl.BlockSpec(memory_space=pltpu.VMEM)
    smem = pl.BlockSpec(memory_space=pltpu.SMEM)
    hbm = pl.BlockSpec(memory_space=pl.ANY)
    dma = pltpu.SemaphoreType.DMA
    merged, outgoing = pl.pallas_call(
        kernel,
        out_shape=(
            pltpu.VMEM((2, rows, width), jnp.bfloat16),
            pltpu.VMEM((2, rows), jnp.float32),
        ),
        in_specs=[smem, smem, hbm, hbm, hbm],
        out_specs=(vmem, vmem),
        scratch_shapes=[
            pltpu.VMEM((2, panel, width), jnp.bfloat16),
            pltpu.VMEM((1, width), jnp.int32),
            pltpu.VMEM((width, width), jnp.bfloat16),
            pltpu.VMEM((2, panel, width), jnp.bfloat16),
            pltpu.VMEM((2, width, panel), jnp.bfloat16),
            pltpu.VMEM((4, 2, panel, panel), jnp.bfloat16),
            pltpu.VMEM((STEPS, 2, 2, 2 * grain, panel), jnp.bfloat16),
            pltpu.VMEM((STEPS, 2, 2, 2 * grain, panel), jnp.bfloat16),
            pltpu.VMEM((2, 2, 2, panel, width), jnp.bfloat16),
            pltpu.VMEM((4, 2, width), jnp.float32),
            dma((3,)),
            dma((2, 2)), dma((2, 2)),
            dma((STEPS, 2)), dma((STEPS, 2)),
            dma((STEPS,)), dma((STEPS,)),
            dma((2, STEPS)), dma((2, STEPS)),
            dma((4,)), dma((4,)),
        ],
        compiler_params=pltpu.CompilerParams(
            collective_id=0, has_side_effects=True, vmem_limit_bytes=60 * 1024 * 1024
        ),
    )(order_x.T, order_y.T, leaf, face_index[0], traces[0, 0])
    return (
        merged.reshape(1, 1, 1, 2, rows, width),
        outgoing.reshape(1, 1, 1, 2, rows),
    )


def solution(mesh):
    placed = (
        P("gx", "gy", None, "pa", None),
        P("gx", "gy", None),
        P(),
        P(),
        P("gx", "gy", None, None),
    )
    return jax.shard_map(
        per_device,
        mesh=mesh,
        in_specs=placed,
        out_specs=(P("gx", "gy", "pa", None, None, None), P("gx", "gy", "pa", None, None)),
        check_vma=False,
    )
```
